32 devices in a mesh: run: 8 (over y, x, core), seg: 4 (over z).
Axes of the slice: x: 2, y: 2, z: 4, core: 2. Of those that a mesh axis runs over, the one named last changes fastest.
Arguments:
- diag_blocks: float32 [4, 16, 256, 256], P('seg', 'run'), as said below
- coupling: float32 [4, 16, 256, 256], P('seg', 'run')
- rhs: float32 [4, 16, 256, 128], P('seg', 'run'), may hold values from -0.65 to 0.65
Outputs:
- solution: float32 [4, 16, 256, 128], P('seg', 'run')
The draws below stay inside these ranges and needn't reach their ends.
Inputs may be any that keep to these rules, and one draw needn't show every extreme that they name: Together with coupling, diag_blocks makes A symmetric positive definite.
All inputs are finite; a program needn't handle non-finite values.
Results may differ from the reference program's by a relative error of at most 0.0003.
Values sent between devices are 32-bit elements; how exact they have to be, the bound alone decides.
A program may use at most 128 MiB of HBM per device.

```python
import math
import jax
import jax.numpy as jnp
from jax import lax

B = 256
R = 128
SEGMENTS = 4
SEG_SLABS = 16


def conductances(key):
    slab_total = SEGMENTS * SEG_SLABS
    noise_key = jax.random.fold_in(key, 7)
    noise_raw = jax.random.normal(noise_key, (slab_total, B, B), jnp.float32)
    gram_part = jnp.einsum('sij,skj->sik', noise_raw, noise_raw) / B
    return 0.5 * jnp.eye(B, dtype=jnp.float32) + 0.5 * gram_part


def draw_diag_blocks(key, part):
    slab_total = SEGMENTS * SEG_SLABS
    conduct = conductances(key)
    rolled = jnp.roll(conduct, -1, axis=0)
    log_low = math.log(0.001)
    log_high = math.log(0.01)
    masses = jnp.exp(jax.random.uniform(jax.random.fold_in(key, 9), (slab_total, B), jnp.float32, log_low, log_high))
    blocks = conduct + rolled + masses[:, :, None] * jnp.eye(B, dtype=jnp.float32)
    return blocks.reshape(SEGMENTS, SEG_SLABS, B, B)


def draw_coupling(key, part):
    return (-conductances(key)).reshape(SEGMENTS, SEG_SLABS, B, B)


def draw_rhs(key, part):
    slab_total = SEGMENTS * SEG_SLABS
    rough_key = jax.random.fold_in(key, 21)
    rough = jnp.clip(0.1 * jax.random.normal(rough_key, (slab_total, B, R), jnp.float32), -0.6, 0.6)
    amplitude = 0.003
    phase = jax.random.uniform(jax.random.fold_in(key, 22), (), jnp.float32, 0.0, 2.0 * math.pi)
    position = jnp.arange(slab_total, dtype=jnp.float32) / slab_total
    profile = 1.0 + 0.6 * jnp.cos(3.0 * math.pi * position + phase)
    weights = jax.random.uniform(jax.random.fold_in(key, 23), (1, B, R), jnp.float32, 0.5, 1.5)
    values = rough + amplitude * profile[:, None, None] * weights
    return values.reshape(SEGMENTS, SEG_SLABS, B, R)


def setup_inputs(seed: int = 0) -> dict:
    seeds = jax.random.split(jax.random.key(seed), 4)
    diag_blocks = draw_diag_blocks(jax.random.fold_in(seeds[3], 71), 0)
    coupling = draw_coupling(jax.random.fold_in(seeds[3], 71), 0)
    rhs = draw_rhs(jax.random.fold_in(seeds[3], 71), 0)
    return {"diag_blocks": diag_blocks, "coupling": coupling, "rhs": rhs}


HIGH = lax.Precision.HIGHEST

def product(operand, second):
    return jnp.dot(operand, second, precision=HIGH, preferred_element_type=operand.dtype)

def apply_inverse(factor, columns):
    return jax.scipy.linalg.cho_solve((factor, True), columns)

def reference(diag_blocks, coupling, rhs):
    order_b = diag_blocks.shape[-1]
    slab_total = diag_blocks.shape[0] * diag_blocks.shape[1]
    diagonal = diag_blocks.reshape(slab_total, order_b, order_b)
    couples = coupling.reshape(slab_total, order_b, order_b)
    couples = couples.at[0].set(jnp.zeros_like(couples[0]))
    sources = rhs.reshape(slab_total, order_b, rhs.shape[-1])
    couples_after = jnp.concatenate([couples[1:], jnp.zeros_like(couples[:1])], axis=0)

    def forward(state_now, slab_item):
        solved_link, solved_prev = state_now
        diag_here, coup_here, coup_next, source_here = slab_item
        factor = jnp.linalg.cholesky(diag_here - product(coup_here, solved_link))
        link_here = apply_inverse(factor, coup_next.T)
        value_here = apply_inverse(factor, source_here - product(coup_here, solved_prev))
        return ((link_here, value_here), (link_here, value_here))
    initial = (jnp.zeros_like(diagonal[0]), jnp.zeros_like(sources[0]))
    _, (links, partials) = lax.scan(forward, initial, (diagonal, couples, couples_after, sources))

    def backward(later, slab_item):
        link_here, partial_value = slab_item
        result = partial_value - product(link_here, later)
        return (result, result)
    _, values = lax.scan(backward, jnp.zeros_like(sources[0]), (links, partials), reverse=True)
    return values.reshape(rhs.shape)
```

```python
import jax
import jax.numpy as jnp
from jax import lax
from jax.experimental import pallas as pl
from jax.experimental.pallas import tpu as pltpu
from jax.sharding import PartitionSpec as P

HIGH = lax.Precision.HIGHEST
ROWS = 8
LANES = 128


def dot(a, b):
    return jnp.dot(a, b, precision=HIGH, preferred_element_type=jnp.float32)


def spd_inverse_tile(rows):
    count = len(rows)
    width = rows[0].shape[1]
    shape = (ROWS, width)
    sub = lax.broadcasted_iota(jnp.int32, shape, 0)
    lane = lax.broadcasted_iota(jnp.int32, shape, 1)
    rows = list(rows)
    for k in range(count):
        first = k * ROWS
        panel = rows[k]
        cols = [jnp.broadcast_to(panel[:, first + j : first + j + 1], shape) for j in range(ROWS)]
        for j in range(ROWS):
            here = sub == j
            pivot = jnp.broadcast_to(cols[j][j : j + 1, :], shape)
            inverse = 1.0 / pivot
            factor = jnp.where(here, -1.0, cols[j])
            panel = jnp.where(lane == first + j, jnp.where(here, 1.0, 0.0), panel)
            line = jnp.broadcast_to(panel[j : j + 1, :], shape)
            panel = jnp.where(here, 0.0, panel) - (factor * line) * inverse
            for m in range(j + 1, ROWS):
                line = jnp.broadcast_to(cols[m][j : j + 1, :], shape)
                cols[m] = jnp.where(here, 0.0, cols[m]) - (factor * line) * inverse
        lines = [jnp.broadcast_to(panel[j : j + 1, :], shape) for j in range(ROWS)]
        inside = jnp.logical_and(lane >= first, lane < first + ROWS)
        for i in range(count):
            if i == k:
                continue
            old = rows[i]
            terms = [
                jnp.broadcast_to(old[:, first + j : first + j + 1], shape) * lines[j]
                for j in range(ROWS)
            ]
            while len(terms) > 1:
                terms = [terms[t] + terms[t + 1] for t in range(0, len(terms), 2)]
            rows[i] = jnp.where(inside, 0.0, old) - terms[0]
        rows[k] = panel
    return rows


def invert_into(d_ref, x_ref, tile_ref, side_ref):
    order = d_ref.shape[0]
    blocks = order // LANES
    x_ref[...] = d_ref[...]

    @pl.loop(0, blocks)
    def _(step):
        for at in range(blocks):

            @pl.when(step == at)
            def _():
                own = slice(at * LANES, (at + 1) * LANES)
                tile_ref[...] = x_ref[own, own]

        tile = spd_inverse_tile([tile_ref[i : i + ROWS, :] for i in range(0, LANES, ROWS)])
        for i, row in enumerate(tile):
            tile_ref[i * ROWS : (i + 1) * ROWS, :] = row

        for at in range(blocks):

            @pl.when(step == at)
            def _():
                own = slice(at * LANES, (at + 1) * LANES)
                inverse = tile_ref[...]
                for other in range(blocks):
                    if other != at:
                        theirs = slice(other * LANES, (other + 1) * LANES)
                        side_ref[own, theirs] = dot(inverse, x_ref[own, theirs])
                for other in range(blocks):
                    if other == at:
                        continue
                    theirs = slice(other * LANES, (other + 1) * LANES)
                    link = x_ref[theirs, own]
                    for last in range(blocks):
                        if last != at:
                            there = slice(last * LANES, (last + 1) * LANES)
                            x_ref[theirs, there] = x_ref[theirs, there] - dot(
                                link, side_ref[own, there]
                            )
                    x_ref[theirs, own] = -dot(link, inverse)
                for other in range(blocks):
                    if other != at:
                        theirs = slice(other * LANES, (other + 1) * LANES)
                        x_ref[own, theirs] = side_ref[own, theirs]
                x_ref[own, own] = inverse


def eliminate_kernel(d, e, f, b, w_e, w_f, y, d_a, d_c, up, low, b_a, b_c, x, tile, side):
    invert_into(d, x, tile, side)
    inverse = x[...]
    e_turned = e[...].T
    f_turned = f[...].T
    w_e[...] = dot(inverse, e[...])
    w_f[...] = dot(inverse, f[...])
    y[...] = dot(inverse, b[...])
    d_a[...] = -dot(e_turned, w_e[...])
    d_c[...] = -dot(f_turned, w_f[...])
    up[...] = -dot(e_turned, w_f[...])
    low[...] = -dot(f_turned, w_e[...])
    b_a[...] = -dot(e_turned, y[...])
    b_c[...] = -dot(f_turned, y[...])


def eliminate(d, e, f, b):
    square = jax.ShapeDtypeStruct(d.shape, jnp.float32)
    thin = jax.ShapeDtypeStruct(b.shape, jnp.float32)
    return pl.pallas_call(
        eliminate_kernel,
        out_shape=(square, square, thin, square, square, square, square, thin, thin),
        scratch_shapes=[
            pltpu.VMEM(d.shape, jnp.float32),
            pltpu.VMEM((LANES, LANES), jnp.float32),
            pltpu.VMEM(d.shape, jnp.float32),
        ],
        name="eliminate",
    )(d, e, f, b)


def solve_kernel(d, b, y, x, tile, side):
    invert_into(d, x, tile, side)
    y[...] = dot(x[...], b[...])


def solve_root(d, b):
    return pl.pallas_call(
        solve_kernel,
        out_shape=jax.ShapeDtypeStruct(b.shape, jnp.float32),
        scratch_shapes=[
            pltpu.VMEM(d.shape, jnp.float32),
            pltpu.VMEM((LANES, LANES), jnp.float32),
            pltpu.VMEM(d.shape, jnp.float32),
        ],
        name="root",
    )(d, b)


AXES = ("run", "seg")


def local(diag_blocks, coupling, rhs):
    diagonal, couples, sources = diag_blocks[0], coupling[0], rhs[0]
    slabs = diagonal.shape[0]
    run_count = lax.axis_size("run")
    total = run_count * lax.axis_size("seg")
    me = lax.axis_index("seg") * run_count + lax.axis_index("run")

    def moved(values, pairs):
        place = lambda g: (g % run_count) * (total // run_count) + g // run_count
        return lax.ppermute(values, AXES, [(place(a), place(b)) for a, b in pairs])

    link = jnp.where(me == 0, 0.0, couples[0])
    node, source = diagonal[0], sources[0]
    saved = []
    prev_diag = prev_source = 0.0
    for i in range(slabs - 1):
        w_e, w_f, y, d_a, d_c, up, low, b_a, b_c = eliminate(node, link, couples[i + 1].T, source)
        saved.append((w_e, w_f, y))
        prev_diag, prev_source, prev_up = prev_diag + d_a, prev_source + b_a, up
        node, source, link = diagonal[i + 1] + d_c, sources[i + 1] + b_c, low
    down = [(g, g - 1) for g in range(1, total)]
    got_diag, got_source, upper = moved((prev_diag, prev_source, prev_up), down)
    node, source = node + got_diag, source + got_source

    levels = []
    stride = 1
    while stride < total:
        gone = list(range(stride - 1, total, 2 * stride))
        w_e, w_f, y, d_a, d_c, up, low, b_a, b_c = eliminate(node, link, upper, source)
        levels.append((stride, gone, w_e, w_f, y))
        got_d, got_b, upper_new = moved(
            (d_a, b_a, up), [(g, g - stride) for g in gone if g - stride >= 0]
        )
        also_d, also_b, link_new = moved((d_c, b_c, low), [(g, g + stride) for g in gone])
        node, source = node + got_d + also_d, source + got_b + also_b
        link, upper = link_new, upper_new
        stride *= 2
    value = solve_root(node, source)
    for stride, gone, w_e, w_f, y in reversed(levels):
        above = moved(value, [(g + stride, g) for g in gone])
        below = moved(value, [(g - stride, g) for g in gone if g - stride >= 0])
        fresh = y - dot(w_e, below) - dot(w_f, above)
        value = jnp.where(lax.rem(me, 2 * stride) == stride - 1, fresh, value)
    before = moved(value, [(g, g + 1) for g in range(total - 1)])
    result = [value]
    for w_e, w_f, y in reversed(saved):
        result.insert(0, y - dot(w_e, before) - dot(w_f, result[0]))
    return jnp.stack(result)[None]


def solution(mesh):
    spec = P("seg", "run", None, None)
    return jax.shard_map(
        local, mesh=mesh, in_specs=(spec, spec, spec), out_specs=spec, check_vma=False
    )
```

```python
import functools

import jax
import jax.numpy as jnp
from jax import lax
from jax.experimental import pallas as pl
from jax.experimental.pallas import tpu as pltpu
from jax.sharding import PartitionSpec as P

MESH = pl.DeviceIdType.MESH
HIGH = lax.Precision.HIGHEST
ROWS = 8
LANES = 128


def dot(a, b):
    return jnp.dot(a, b, precision=HIGH, preferred_element_type=jnp.float32)


def spd_inverse_tile(rows):
    count = len(rows)
    width = rows[0].shape[1]
    shape = (ROWS, width)
    sub = lax.broadcasted_iota(jnp.int32, shape, 0)
    lane = lax.broadcasted_iota(jnp.int32, shape, 1)
    rows = list(rows)
    for k in range(count):
        first = k * ROWS
        panel = rows[k]
        cols = [jnp.broadcast_to(panel[:, first + j : first + j + 1], shape) for j in range(ROWS)]
        for j in range(ROWS):
            here = sub == j
            pivot = jnp.broadcast_to(cols[j][j : j + 1, :], shape)
            inverse = 1.0 / pivot
            factor = jnp.where(here, -1.0, cols[j])
            panel = jnp.where(lane == first + j, jnp.where(here, 1.0, 0.0), panel)
            line = jnp.broadcast_to(panel[j : j + 1, :], shape)
            panel = jnp.where(here, 0.0, panel) - (factor * line) * inverse
            for m in range(j + 1, ROWS):
                line = jnp.broadcast_to(cols[m][j : j + 1, :], shape)
                cols[m] = jnp.where(here, 0.0, cols[m]) - (factor * line) * inverse
        lines = [jnp.broadcast_to(panel[j : j + 1, :], shape) for j in range(ROWS)]
        inside = jnp.logical_and(lane >= first, lane < first + ROWS)
        for i in range(count):
            if i == k:
                continue
            old = rows[i]
            terms = [
                jnp.broadcast_to(old[:, first + j : first + j + 1], shape) * lines[j]
                for j in range(ROWS)
            ]
            while len(terms) > 1:
                terms = [terms[t] + terms[t + 1] for t in range(0, len(terms), 2)]
            rows[i] = jnp.where(inside, 0.0, old) - terms[0]
        rows[k] = panel
    return rows


def invert_into(d_ref, x_ref, tile_ref, side_ref):
    order = d_ref.shape[0]
    blocks = order // LANES
    x_ref[...] = d_ref[...]

    @pl.loop(0, blocks)
    def _(step):
        for at in range(blocks):

            @pl.when(step == at)
            def _():
                own = slice(at * LANES, (at + 1) * LANES)
                tile_ref[...] = x_ref[own, own]

        tile = spd_inverse_tile([tile_ref[i : i + ROWS, :] for i in range(0, LANES, ROWS)])
        for i, row in enumerate(tile):
            tile_ref[i * ROWS : (i + 1) * ROWS, :] = row

        for at in range(blocks):

            @pl.when(step == at)
            def _():
                own = slice(at * LANES, (at + 1) * LANES)
                inverse = tile_ref[...]
                for other in range(blocks):
                    if other != at:
                        theirs = slice(other * LANES, (other + 1) * LANES)
                        side_ref[own, theirs] = dot(inverse, x_ref[own, theirs])
                for other in range(blocks):
                    if other == at:
                        continue
                    theirs = slice(other * LANES, (other + 1) * LANES)
                    link = x_ref[theirs, own]
                    for last in range(blocks):
                        if last != at:
                            there = slice(last * LANES, (last + 1) * LANES)
                            x_ref[theirs, there] = x_ref[theirs, there] - dot(
                                link, side_ref[own, there]
                            )
                    x_ref[theirs, own] = -dot(link, inverse)
                for other in range(blocks):
                    if other != at:
                        theirs = slice(other * LANES, (other + 1) * LANES)
                        x_ref[own, theirs] = side_ref[own, theirs]
                x_ref[own, own] = inverse


def kernel(
    runs,
    total,
    diag,
    coup,
    rhs,
    out,
    x,
    tile,
    side,
    node,
    source,
    link,
    turned,
    keep_e,
    keep_f,
    keep_y,
    send_d,
    send_m,
    send_b,
    first_d,
    first_b,
    got_d,
    got_b,
    got_low,
    got_up,
    above,
    below,
    before,
    value,
    sent,
    sent_first,
    sent_value,
    come_d,
    come_b,
    come_m,
    come_first,
    come_value,
):
    slabs = diag.shape[0]
    inner = slabs - 1
    me = lax.axis_index("seg") * runs + lax.axis_index("run")
    strides = [1 << i for i in range(total.bit_length() - 1)]
    root = me == total - 1
    even = lax.rem(me, 2) == 0

    def copy(source_ref, target_ref, send_sem, recv_sem, peer):
        return pltpu.make_async_remote_copy(
            src_ref=source_ref,
            dst_ref=target_ref,
            send_sem=send_sem,
            recv_sem=recv_sem,
            device_id=(lax.rem(peer, runs), lax.div(peer, runs)),
            device_id_type=MESH,
        )

    barrier = pltpu.get_barrier_semaphore()
    met = [lax.rem(me + 1, s) == 0 for s in strides]
    peers = sum(
        jnp.where(jnp.logical_and(here, ok), 1, 0)
        for s, here in zip(strides, met)
        for ok in (me >= s, me + s < total)
    )
    for s, here in zip(strides, met):
        for ok, peer in ((me >= s, me - s), (me + s < total, me + s)):

            @pl.when(jnp.logical_and(here, ok))
            def _():
                pl.semaphore_signal(
                    barrier,
                    inc=1,
                    device_id=(lax.rem(peer, runs), lax.div(peer, runs)),
                    device_id_type=MESH,
                )

    link[...] = jnp.where(me == 0, jnp.zeros_like(coup[0]), coup[0])
    node[...] = diag[0]
    source[...] = rhs[0]
    for i in range(inner):
        invert_into(node, x, tile, side)
        f_turned = coup[i + 1]
        turned[...] = link[...].T
        keep_e[i] = dot(x[...], link[...])
        keep_f[i] = dot(x[...], f_turned.T)
        term = dot(turned[...], keep_e[i])
        first_d[...] = -term if i == 0 else first_d[...] - term
        node[...] = diag[i + 1] - dot(f_turned, keep_f[i])
        if i == inner - 1:
            pl.semaphore_wait(barrier, peers)

            @pl.when(me > 0)
            def _():
                copy(first_d, got_d.at[0], sent_first.at[0], come_first.at[0], me - 1).start()

            @pl.when(jnp.logical_not(even))
            def _():
                send_m[...] = -dot(turned[...], keep_f[i])
                copy(send_m, got_up, sent_first.at[1], come_m.at[1], me - 1).start()

        keep_y[i] = dot(x[...], source[...])
        term = dot(turned[...], keep_y[i])
        first_b[...] = -term if i == 0 else first_b[...] - term
        if i == inner - 1:

            @pl.when(me > 0)
            def _():
                copy(first_b, got_b.at[0], sent_first.at[2], come_first.at[1], me - 1).start()

        source[...] = rhs[i + 1] - dot(f_turned, keep_y[i])
        link[...] = -dot(f_turned, keep_e[i])

    @pl.when(jnp.logical_not(root))
    def _():
        copy(first_d, got_d.at[0], sent_first.at[0], come_first.at[0], me + 1).wait_recv()
        node[...] = node[...] + got_d[0]

    for i, s in enumerate(strides):
        for way, (ok, peer) in enumerate(((me >= s, me - s), (me + s < total, me + s))):

            @pl.when(jnp.logical_and(lax.rem(me + 1, 2 * s) == 0, ok))
            def _():
                slot = 1 + 2 * i + way
                copy(
                    first_d, got_d.at[slot], sent_first.at[0], come_d.at[2 * i + way], peer
                ).wait_recv()
                node[...] = node[...] + got_d[slot]

    @pl.when(jnp.logical_not(even))
    def _():
        copy(send_m, got_up, sent_first.at[1], come_m.at[1], me - 1).wait_send()

    invert_into(node, x, tile, side)

    @pl.when(jnp.logical_not(root))
    def _():
        copy(first_b, got_b.at[0], sent_first.at[2], come_first.at[1], me + 1).wait_recv()
        source[...] = source[...] + got_b[0]

    for i, s in enumerate(strides):
        for way, (ok, peer) in enumerate(((me >= s, me - s), (me + s < total, me + s))):

            @pl.when(jnp.logical_and(lax.rem(me + 1, 2 * s) == 0, ok))
            def _():
                slot = 1 + 2 * i + way
                copy(
                    first_b, got_b.at[slot], sent_first.at[2], come_b.at[2 * i + way], peer
                ).wait_recv()
                source[...] = source[...] + got_b[slot]

    @pl.when(jnp.logical_not(root))
    def _():
        copy(send_m, got_up, sent_first.at[1], come_m.at[1], me + 1).wait_recv()

        @pl.when(jnp.logical_not(even))
        def _():
            copy(send_m, got_low, sent_first.at[1], come_m.at[0], me - 1).wait_recv()
            link[...] = got_low[...]

        turned[...] = got_up[...].T
        keep_f[inner] = dot(x[...], got_up[...])
        send_d[1] = -dot(turned[...], keep_f[inner])

    def sends(stage, act):
        for i, s in enumerate(strides):
            mine = lax.rem(me, 2 * s) == s - 1
            lower = jnp.logical_and(mine, me >= s)
            to_low = jnp.logical_and(lax.rem(me + s, 4 * s) == 2 * s - 1, me + s < total - 1)
            if stage == "up":

                @pl.when(mine)
                def _():
                    act(copy(send_d.at[1], got_d.at[1 + 2 * i], sent.at[0], come_d.at[2 * i], me + s))

            if stage == "down":

                @pl.when(lower)
                def _():
                    act(
                        copy(
                            send_d.at[0],
                            got_d.at[2 + 2 * i],
                            sent.at[1],
                            come_d.at[2 * i + 1],
                            me - s,
                        )
                    )

            if stage == "link":

                @pl.when(jnp.logical_and(mine, to_low))
                def _():
                    act(copy(send_m, got_low, sent.at[2], come_m.at[0], me + s))

                @pl.when(jnp.logical_and(lower, lax.rem(me + s, 4 * s) == 4 * s - 1))
                def _():
                    act(copy(send_m, got_up, sent.at[2], come_m.at[1], me - s))

            if stage == "thin":

                @pl.when(mine)
                def _():
                    act(copy(send_b.at[1], got_b.at[1 + 2 * i], sent.at[3], come_b.at[2 * i], me + s))

                @pl.when(lower)
                def _():
                    act(
                        copy(
                            send_b.at[0],
                            got_b.at[2 + 2 * i],
                            sent.at[4],
                            come_b.at[2 * i + 1],
                            me - s,
                        )
                    )

    start = lambda c: c.start()
    done = lambda c: c.wait_send()
    sends("up", start)

    @pl.when(jnp.logical_not(root))
    def _():
        side[...] = link[...].T
        keep_e[inner] = dot(x[...], link[...])
        send_d[0] = -dot(side[...], keep_e[inner])

    sends("down", start)
    next_above = functools.reduce(
        jnp.logical_or,
        [
            jnp.logical_and(
                lax.rem(me, 2 * s) == s - 1, lax.rem(me + s, 4 * s) == 2 * s - 1
            )
            for s in strides
        ],
    )

    @pl.when(next_above)
    def _():
        send_m[...] = -dot(turned[...], keep_e[inner])

    @pl.when(jnp.logical_not(next_above))
    def _():
        send_m[...] = -dot(side[...], keep_f[inner])

    sends("link", start)
    keep_y[inner] = dot(x[...], source[...])
    value[...] = keep_y[inner]

    @pl.when(jnp.logical_not(root))
    def _():
        send_b[1] = -dot(turned[...], keep_y[inner])
        send_b[0] = -dot(side[...], keep_y[inner])

    sends("thin", start)

    for i, s in enumerate(strides):
        mine = lax.rem(me, 2 * s) == s - 1

        @pl.when(jnp.logical_and(mine, me >= s))
        def _():
            copy(value, below, sent_value.at[0], come_value.at[0], me - s).wait_recv()
            value[...] = value[...] - dot(keep_e[inner], below[...])

        @pl.when(mine)
        def _():
            copy(value, above, sent_value.at[0], come_value.at[1], me + s).wait_recv()
            value[...] = value[...] - dot(keep_f[inner], above[...])

    def hand_down(act):
        for i, s in reversed(list(enumerate(strides))):
            parent = lax.rem(me + 1, 2 * s) == 0

            @pl.when(parent)
            def _():
                act(copy(value, above, sent_value.at[2 * i], come_value.at[1], me - s))

            @pl.when(jnp.logical_and(parent, me + s < total))
            def _():
                act(copy(value, below, sent_value.at[2 * i + 1], come_value.at[0], me + s))

        @pl.when(even)
        def _():
            act(copy(value, before, sent_value.at[2 * len(strides)], come_value.at[2], me + 1))

    hand_down(start)
    out[inner] = value[...]
    for i in reversed(range(inner)):
        out[i] = keep_y[i] - dot(keep_f[i], out[i + 1])

    @pl.when(jnp.logical_and(even, me > 0))
    def _():
        for i in reversed(range(inner)):
            out[i] = out[i] - dot(keep_e[i], below[...])

    @pl.when(jnp.logical_not(even))
    def _():
        copy(value, before, sent_value.at[2 * len(strides)], come_value.at[2], me - 1).wait_recv()
        for i in reversed(range(inner)):
            out[i] = out[i] - dot(keep_e[i], before[...])

    for stage in ("up", "down", "link", "thin"):
        sends(stage, done)
    hand_down(done)

    @pl.when(me > 0)
    def _():
        copy(first_d, got_d.at[0], sent_first.at[0], come_first.at[0], me - 1).wait_send()
        copy(first_b, got_b.at[0], sent_first.at[2], come_first.at[1], me - 1).wait_send()


def local(runs, total, diag_blocks, coupling, rhs):
    slabs, order = diag_blocks.shape[1:3]
    columns = rhs.shape[3]
    depth = total.bit_length() - 1
    square, thin = (order, order), (order, columns)
    vmem = lambda *shape: pltpu.VMEM(shape, jnp.float32)
    dma = lambda n: pltpu.SemaphoreType.DMA((n,))
    result = pl.pallas_call(
        functools.partial(kernel, runs, total),
        out_shape=jax.ShapeDtypeStruct(rhs.shape[1:], jnp.float32),
        in_specs=[pl.BlockSpec(memory_space=pltpu.VMEM)] * 3,
        out_specs=pl.BlockSpec(memory_space=pltpu.VMEM),
        scratch_shapes=[
            vmem(*square),
            vmem(LANES, LANES),
            vmem(*square),
            vmem(*square),
            vmem(*thin),
            vmem(*square),
            vmem(*square),
            vmem(slabs, *square),
            vmem(slabs, *square),
            vmem(slabs, *thin),
            vmem(2, *square),
            vmem(*square),
            vmem(2, *thin),
            vmem(*square),
            vmem(*thin),
            vmem(1 + 2 * depth, *square),
            vmem(1 + 2 * depth, *thin),
            vmem(*square),
            vmem(*square),
            vmem(*thin),
            vmem(*thin),
            vmem(*thin),
            vmem(*thin),
            dma(5),
            dma(3),
            dma(2 * depth + 1),
            dma(2 * depth),
            dma(2 * depth),
            dma(2),
            dma(2),
            dma(3),
        ],
        compiler_params=pltpu.CompilerParams(collective_id=0, has_side_effects=True),
        name="chain_solve",
    )(diag_blocks[0], coupling[0], rhs[0])
    return result[None]


def solution(mesh):
    spec = P("seg", "run", None, None)
    runs = mesh.shape["run"]
    total = runs * mesh.shape["seg"]
    return jax.shard_map(
        functools.partial(local, runs, total),
        mesh=mesh,
        in_specs=(spec, spec, spec),
        out_specs=spec,
        check_vma=False,
    )
```

```python
import functools

import jax
import jax.numpy as jnp
from jax import lax
from jax.experimental import pallas as pl
from jax.experimental.pallas import tpu as pltpu
from jax.sharding import PartitionSpec as P

MESH = pl.DeviceIdType.MESH
HIGH = lax.Precision.HIGHEST
ROWS = 8
LANES = 128


def dot(a, b):
    return jnp.dot(a, b, precision=HIGH, preferred_element_type=jnp.float32)


def dot_nt(a, b):
    return lax.dot_general(
        a, b, (((1,), (1,)), ((), ())), precision=HIGH, preferred_element_type=jnp.float32
    )


def spd_inverse_tile(rows):
    count = len(rows)
    width = rows[0].shape[1]
    shape = (ROWS, width)
    sub = lax.broadcasted_iota(jnp.int32, shape, 0)
    lane = lax.broadcasted_iota(jnp.int32, shape, 1)
    rows = list(rows)
    for k in range(count):
        first = k * ROWS
        panel = rows[k]
        cols = [jnp.broadcast_to(panel[:, first + j : first + j + 1], shape) for j in range(ROWS)]
        for j in range(ROWS):
            here = sub == j
            pivot = jnp.broadcast_to(cols[j][j : j + 1, :], shape)
            inverse = 1.0 / pivot
            factor = jnp.where(here, -1.0, cols[j])
            panel = jnp.where(lane == first + j, jnp.where(here, 1.0, 0.0), panel)
            line = jnp.broadcast_to(panel[j : j + 1, :], shape)
            panel = jnp.where(here, 0.0, panel) - (factor * line) * inverse
            for m in range(j + 1, ROWS):
                line = jnp.broadcast_to(cols[m][j : j + 1, :], shape)
                cols[m] = jnp.where(here, 0.0, cols[m]) - (factor * line) * inverse
        lines = [jnp.broadcast_to(panel[j : j + 1, :], shape) for j in range(ROWS)]
        inside = jnp.logical_and(lane >= first, lane < first + ROWS)
        for i in range(count):
            if i == k:
                continue
            old = rows[i]
            terms = [
                jnp.broadcast_to(old[:, first + j : first + j + 1], shape) * lines[j]
                for j in range(ROWS)
            ]
            while len(terms) > 1:
                terms = [terms[t] + terms[t + 1] for t in range(0, len(terms), 2)]
            rows[i] = jnp.where(inside, 0.0, old) - terms[0]
        rows[k] = panel
    return rows


def invert(node, x, tile, work, late):
    half = tile.shape[0]
    top, low = slice(0, half), slice(half, 2 * half)
    tile[...] = node[0]

    @pl.loop(0, 2)
    def _(step):
        rows = spd_inverse_tile([tile[i : i + ROWS, :] for i in range(0, half, ROWS)])
        for i, row in enumerate(rows):
            tile[i * ROWS : (i + 1) * ROWS, :] = row

        @pl.when(step == 0)
        def _():
            late()
            x[top, top] = tile[...]
            work[0] = dot(tile[...], node[1])
            work[1] = work[0].T
            tile[...] = node[2] - dot(work[1], node[1])

        @pl.when(step == 1)
        def _():
            corner = -dot(tile[...], work[1])
            x[low, low] = tile[...]
            x[low, top] = corner
            x[top, low] = -dot(work[0], tile[...])
            x[top, top] = x[top, top] - dot(work[0], corner)


def kernel(
    runs,
    total,
    diag,
    coup,
    rhs,
    out,
    x,
    tile,
    work,
    node,
    source,
    e_turned,
    w_p,
    w_q,
    keep_p,
    keep_q,
    keep_y,
    send_d,
    send_m,
    send_b,
    first_d,
    first_b,
    got_d,
    got_b,
    got_link,
    got_x,
    before,
    value,
    sent,
    sent_first,
    sent_value,
    come_d,
    come_b,
    come_m,
    come_x,
):
    slabs, order = diag.shape[:2]
    inner = slabs - 1
    half = order // 2
    top, low = slice(0, half), slice(half, order)
    me = lax.axis_index("seg") * runs + lax.axis_index("run")
    depth = total.bit_length() - 1
    strides = [1 << i for i in range(depth)]
    root = me == total - 1
    inside = jnp.logical_not(root)
    even = lax.rem(me, 2) == 0
    odd = jnp.logical_not(even)
    parents = [lax.rem(me + 1, 2 * s) == 0 for s in strides]
    level = sum(jnp.where(parent, 1, 0) for parent in parents)
    span = 1 + sum(jnp.where(parent, s, 0) for s, parent in zip(strides, parents))
    next_above = lax.rem(me + span, 4 * span) == 2 * span - 1
    up = jnp.where(next_above, 1, 0)
    peer_p = jnp.where(next_above, me + span, me - span)
    peer_q = jnp.where(next_above, me - span, me + span)
    has_q = jnp.logical_and(inside, jnp.logical_and(peer_q >= 0, peer_q < total))
    slot_p = 1 + 2 * level + (1 - up)
    slot_q = 1 + 2 * level + up

    def copy(source_ref, target_ref, send_sem, recv_sem, peer):
        return pltpu.make_async_remote_copy(
            src_ref=source_ref,
            dst_ref=target_ref,
            send_sem=send_sem,
            recv_sem=recv_sem,
            device_id=(lax.rem(peer, runs), lax.div(peer, runs)),
            device_id_type=MESH,
        )

    barrier = pltpu.get_barrier_semaphore()
    met = [lax.rem(me + 1, s) == 0 for s in strides]
    peers = sum(
        jnp.where(jnp.logical_and(here, ok), 1, 0)
        for s, here in zip(strides, met)
        for ok in (me >= s, me + s < total)
    )
    for s, here in zip(strides, met):
        for ok, peer in ((me >= s, me - s), (me + s < total, me + s)):

            @pl.when(jnp.logical_and(here, ok))
            def _():
                pl.semaphore_signal(
                    barrier,
                    inc=1,
                    device_id=(lax.rem(peer, runs), lax.div(peer, runs)),
                    device_id_type=MESH,
                )

    def first_head(peer):
        return copy(first_d.at[0], got_d.at[0, 0], sent_first.at[0], come_d.at[0], peer)

    def first_tail(peer):
        return copy(
            first_d.at[pl.ds(1, 2)], got_d.at[0, pl.ds(1, 2)], sent_first.at[1], come_d.at[1], peer
        )

    def first_link(peer):
        return copy(send_m, got_link.at[1], sent_first.at[2], come_m.at[1], peer)

    def first_thin(peer):
        return copy(first_b, got_b.at[0], sent_first.at[3], come_b.at[0], peer)

    def head(role, slot, peer):
        return copy(
            send_d.at[role, 0], got_d.at[slot, 0], sent.at[role], come_d.at[2 * slot], peer
        )

    def tail(role, slot, peer):
        return copy(
            send_d.at[role, pl.ds(1, 2)],
            got_d.at[slot, pl.ds(1, 2)],
            sent.at[2 + role],
            come_d.at[2 * slot + 1],
            peer,
        )

    def thin(role, slot, peer):
        return copy(send_b.at[role], got_b.at[slot], sent.at[4 + role], come_b.at[slot], peer)

    def coupled(side, peer):
        return copy(send_m, got_link.at[side], sent.at[6], come_m.at[side], peer)

    def each_source(act):
        @pl.when(inside)
        def _():
            act(0, me + 1)

        for i, s in enumerate(strides):
            for way, (ok, peer) in enumerate(((me >= s, me - s), (me + s < total, me + s))):

                @pl.when(jnp.logical_and(parents[i], ok))
                def _():
                    act(1 + 2 * i + way, peer)

    e_turned[...] = jnp.where(me == 0, jnp.zeros_like(coup[0]), coup[0]).T
    node[0] = diag[0, top, top]
    node[1] = diag[0, top, low]
    node[2] = diag[0, low, low]
    source[...] = rhs[0]
    for i in range(inner):
        final = i == inner - 1
        f_turned = coup.at[i + 1]
        invert(node, x, tile, work, lambda: None)
        w_p[...] = dot(e_turned[...], x[...])

        def put(block, rows, columns):
            term = dot_nt(w_p[rows, :], e_turned[columns, :])
            first_d[block] = -term if i == 0 else first_d[block] - term

        put(0, top, top)
        if final:
            pl.semaphore_wait(barrier, peers)

            @pl.when(me > 0)
            def _():
                first_head(me - 1).start()

        put(1, top, low)
        put(2, low, low)
        if final:

            @pl.when(me > 0)
            def _():
                first_tail(me - 1).start()

        w_q[...] = dot(f_turned[...], x[...])
        node[0] = diag[i + 1, top, top] - dot_nt(w_q[top, :], f_turned[top, :])
        node[1] = diag[i + 1, top, low] - dot_nt(w_q[top, :], f_turned[low, :])
        node[2] = diag[i + 1, low, low] - dot_nt(w_q[low, :], f_turned[low, :])
        if final:

            @pl.when(odd)
            def _():
                send_m[...] = -dot_nt(w_q[...], e_turned[...])
                first_link(me - 1).start()

            @pl.when(even)
            def _():
                got_link[0] = -dot_nt(w_p[...], f_turned[...])

        keep_y[i] = dot(x[...], source[...])
        term = dot(e_turned[...], keep_y[i])
        first_b[...] = -term if i == 0 else first_b[...] - term
        if final:

            @pl.when(me > 0)
            def _():
                first_thin(me - 1).start()

        source[...] = rhs[i + 1] - dot(f_turned[...], keep_y[i])
        keep_p[i] = dot_nt(x[...], e_turned[...])
        keep_q[i] = dot_nt(x[...], f_turned[...])
        if not final:
            e_turned[...] = -dot_nt(w_p[...], f_turned[...])

    def add_head(slot, peer):
        head(0, slot, peer).wait_recv()
        node[0] = node[0] + got_d[slot, 0]

    def add_tail(slot, peer):
        tail(0, slot, peer).wait_recv()
        node[1] = node[1] + got_d[slot, 1]
        node[2] = node[2] + got_d[slot, 2]

    def add_thin(slot, peer):
        thin(0, slot, peer).wait_recv()
        source[...] = source[...] + got_b[slot]

    each_source(add_head)
    invert(node, x, tile, work, lambda: each_source(add_tail))

    @pl.when(inside)
    def _():
        coupled(1, me + 1).wait_recv()

        @pl.when(odd)
        def _():
            coupled(0, me - 1).wait_recv()
            first_link(me - 1).wait_send()

        def serve(role, slot, peer, weights, turned):
            weights[top, :] = dot(turned[top, :], x[...])
            send_d[role, 0] = -dot_nt(weights[top, :], turned[top, :])
            go = inside if role == 0 else has_q

            @pl.when(go)
            def _():
                head(role, slot, peer).start()

            send_d[role, 1] = -dot_nt(weights[top, :], turned[low, :])
            weights[low, :] = dot(turned[low, :], x[...])
            send_d[role, 2] = -dot_nt(weights[low, :], turned[low, :])

            @pl.when(go)
            def _():
                tail(role, slot, peer).start()

        serve(0, slot_p, peer_p, w_p, got_link.at[up])
        serve(1, slot_q, peer_q, w_q, got_link.at[1 - up])

        @pl.when(peer_p < total - 1)
        def _():
            send_m[...] = -dot_nt(w_q[...], got_link[up])
            coupled(1 - up, peer_p).start()

    each_source(add_thin)
    keep_y[inner] = dot(x[...], source[...])
    value[...] = keep_y[inner]

    @pl.when(inside)
    def _():
        send_b[0] = -dot(got_link[up], keep_y[inner])
        thin(0, slot_p, peer_p).start()

        @pl.when(has_q)
        def _():
            send_b[1] = -dot(got_link[1 - up], keep_y[inner])
            thin(1, slot_q, peer_q).start()

        keep_p[inner] = dot_nt(x[...], got_link[up])
        keep_q[inner] = dot_nt(x[...], got_link[1 - up])

        @pl.when(has_q)
        def _():
            copy(value, got_x.at[1], sent_value.at[0], come_x.at[1], peer_q).wait_recv()
            value[...] = value[...] - dot(keep_q[inner], got_x[1])

        copy(value, got_x.at[0], sent_value.at[0], come_x.at[0], peer_p).wait_recv()
        value[...] = value[...] - dot(keep_p[inner], got_x[0])

    def hand_down(act):
        for i, s in reversed(list(enumerate(strides))):
            role = jnp.where(level == i + 1, 0, 1)
            for way, (ok, peer) in enumerate(((me >= s, me - s), (me + s < total, me + s))):

                @pl.when(jnp.logical_and(parents[i], ok))
                def _():
                    act(
                        copy(
                            value, got_x.at[role], sent_value.at[2 * i + way], come_x.at[role], peer
                        )
                    )

        @pl.when(even)
        def _():
            act(copy(value, before, sent_value.at[2 * depth], come_x.at[2], me + 1))

    hand_down(lambda c: c.start())
    out[inner] = value[...]
    for i in reversed(range(inner)):
        out[i] = keep_y[i] - dot(keep_q[i], out[i + 1])

    @pl.when(jnp.logical_and(even, me > 0))
    def _():
        for i in reversed(range(inner)):
            out[i] = out[i] - dot(keep_p[i], got_x[up])

    @pl.when(odd)
    def _():
        copy(value, before, sent_value.at[2 * depth], come_x.at[2], me - 1).wait_recv()
        for i in reversed(range(inner)):
            out[i] = out[i] - dot(keep_p[i], before[...])

    @pl.when(inside)
    def _():
        head(0, slot_p, peer_p).wait_send()
        tail(0, slot_p, peer_p).wait_send()
        thin(0, slot_p, peer_p).wait_send()

        @pl.when(peer_p < total - 1)
        def _():
            coupled(1 - up, peer_p).wait_send()

        @pl.when(has_q)
        def _():
            head(1, slot_q, peer_q).wait_send()
            tail(1, slot_q, peer_q).wait_send()
            thin(1, slot_q, peer_q).wait_send()

    hand_down(lambda c: c.wait_send())

    @pl.when(me > 0)
    def _():
        first_head(me - 1).wait_send()
        first_tail(me - 1).wait_send()
        first_thin(me - 1).wait_send()

    @pl.when(jnp.logical_and(odd, root))
    def _():
        first_link(me - 1).wait_send()


def local(runs, total, diag_blocks, coupling, rhs):
    slabs, order = diag_blocks.shape[1:3]
    half = order // 2
    columns = rhs.shape[3]
    depth = total.bit_length() - 1
    square, thin = (order, order), (order, columns)
    vmem = lambda *shape: pltpu.VMEM(shape, jnp.float32)
    dma = lambda n: pltpu.SemaphoreType.DMA((n,))
    slots = 1 + 2 * depth
    result = pl.pallas_call(
        functools.partial(kernel, runs, total),
        out_shape=jax.ShapeDtypeStruct(rhs.shape[1:], jnp.float32),
        in_specs=[pl.BlockSpec(memory_space=pltpu.VMEM)] * 3,
        out_specs=pl.BlockSpec(memory_space=pltpu.VMEM),
        scratch_shapes=[
            vmem(*square),
            vmem(half, half),
            vmem(2, half, half),
            vmem(3, half, half),
            vmem(*thin),
            vmem(*square),
            vmem(*square),
            vmem(*square),
            vmem(slabs, *square),
            vmem(slabs, *square),
            vmem(slabs, *thin),
            vmem(2, 3, half, half),
            vmem(*square),
            vmem(2, *thin),
            vmem(3, half, half),
            vmem(*thin),
            vmem(slots, 3, half, half),
            vmem(slots, *thin),
            vmem(2, *square),
            vmem(2, *thin),
            vmem(*thin),
            vmem(*thin),
            dma(7),
            dma(4),
            dma(slots),
            dma(2 * slots),
            dma(slots),
            dma(2),
            dma(3),
        ],
        compiler_params=pltpu.CompilerParams(collective_id=0, has_side_effects=True),
        name="chain_solve",
    )(diag_blocks[0], coupling[0], rhs[0])
    return result[None]


def solution(mesh):
    spec = P("seg", "run", None, None)
    runs = mesh.shape["run"]
    total = runs * mesh.shape["seg"]
    return jax.shard_map(
        functools.partial(local, runs, total),
        mesh=mesh,
        in_specs=(spec, spec, spec),
        out_specs=spec,
        check_vma=False,
    )
```
